128 devices in a mesh: gx: 16 (over x, y), gy: 8 (over z, core).
Axes of the slice: x: 4, y: 4, z: 4, core: 2. Of those that a mesh axis runs over, the one named last changes fastest.
Arguments:
- estimate: float32 [32, 256, 1024], P(None, 'gx', 'gy'), may hold values from 0.5 to 2
- stored: bfloat16 [16384, 16, 128], P(('gx', 'gy')), may hold values from 0.19921875 to 5
- placement: int32 [16384], replicated, may hold values from 0 to 16383, as said below
- psf_taps: float32 [48, 31], replicated, may hold values from 0.05 to 1
- kernel_index: int32 [16, 8, 4, 3], replicated, may hold values from 0 to 47
Outputs:
- refined: float32 [32, 256, 1024], P(None, 'gx', 'gy')
The draws below stay inside these ranges and needn't reach their ends.
Inputs may be any that keep to these rules, and one draw needn't show every extreme that they name: `placement`: each value occurs once; the value b * 128 + v * 32 + z marks plane z of view v of brick b. Entries d * 128 to (d + 1) * 128 - 1 are the slots of device d of gx+gy; among them at most 2 name any one brick, every device has exactly 2 naming some brick, and every brick has exactly 2 on some device.
All inputs are finite; a program needn't handle non-finite values.
Results may differ from the reference program's by a relative error of at most 0.0003.
Values may be sent and summed in bfloat16 or wider, within the bound.
A program may use at most 128 MiB of HBM per device.

```python
import math
import jax
import jax.numpy as jnp
from jax import lax

BX = 16
BY = 128
NZ = 32
V = 4
TAPS = 31
NK = 48
ITERS = 2
SLOTS = 128
CAP = 2
NX = 256
NY = 1024
N_GX = 16
N_GY = 8
DEVICES = 128


def draw_placement(key, part):
    streams = jax.random.split(jax.random.fold_in(key, 7), 4)
    relabel = jax.random.permutation(streams[0], DEVICES).astype(jnp.int32)
    restore = jnp.argsort(relabel).astype(jnp.int32)
    crowded = jax.random.randint(streams[1], (), 0, DEVICES, dtype=jnp.int32)
    spread = (jax.random.permutation(streams[2], (DEVICES - 1) * CAP)[:SLOTS - CAP] // CAP).astype(jnp.int32)
    spread = spread + (spread >= crowded).astype(jnp.int32)
    offsets = jnp.concatenate([jnp.full((CAP,), crowded, jnp.int32), spread])
    target_brick = restore[(relabel[:, None] - offsets[None, :]) % DEVICES]
    orders = jax.vmap(lambda subkey: jax.random.permutation(subkey, SLOTS))(jax.random.split(streams[3], DEVICES)).astype(jnp.int32)
    plane_item = orders[target_brick, jnp.arange(SLOTS, dtype=jnp.int32)[None, :]]
    return (target_brick * SLOTS + plane_item).reshape(-1).astype(jnp.int32)


def with_ends(result, rng, least, high):
    dims = result.shape
    spot = [jax.random.randint(jax.random.fold_in(rng, axis), (), 0, dims[axis]) for axis in range(len(dims))]
    result = result.at[tuple(spot)].set(least)
    longest = dims.index(max(dims))
    spot[longest] = (spot[longest] + 1) % dims[longest]
    return result.at[tuple(spot)].set(high)


def block_scale(own_key, extent, shards, low, top_value):
    level = 1.0
    for dim, parts in shards:
        steps = jax.random.uniform(jax.random.fold_in(jax.random.fold_in(own_key, 6), dim), (parts,), jnp.float32, low / len(shards), top_value / len(shards))
        level = level * jnp.repeat(jnp.exp(steps), extent[dim] // parts).reshape((-1,) + (1,) * (len(extent) - 1 - dim))
    return level


def setup_inputs(seed: int = 0) -> dict:
    key_list = jax.random.split(jax.random.key(seed), 6)
    estimate = jnp.clip(jnp.exp(math.log(2.0) - 1.3862944 * jax.random.uniform(key_list[0], (NZ, NX, NY), jnp.float32) ** block_scale(key_list[0], (NZ, NX, NY), ((1, 16), (2, 8)), -0.2, 0.2)), 0.5, 2.0)
    stored = jnp.clip(jnp.exp(math.log(5.0) - 3.2227897 * jax.random.uniform(key_list[1], (DEVICES * SLOTS, BX, BY), jnp.float32) ** block_scale(key_list[1], (DEVICES * SLOTS, BX, BY), ((0, 128),), -0.2, 0.2)), 0.19921875, 5.0).astype(jnp.bfloat16)
    placement = draw_placement(jax.random.fold_in(key_list[5], 71), 0)
    psf_taps = jnp.clip(jnp.exp(jax.random.uniform(key_list[3], (NK, TAPS), jnp.float32, math.log(0.05), math.log(1.0))), 0.05, 1.0)
    kernel_index = with_ends(jax.random.randint(key_list[4], (N_GX, N_GY, V, 3), 0, NK), jax.random.fold_in(key_list[4], 1), 0, NK - 1).astype(jnp.int32)
    return dict(estimate=estimate, stored=stored, placement=placement, psf_taps=psf_taps, kernel_index=kernel_index)


precise = lax.Precision.HIGHEST


def lookup(psf_taps, indices):
    chosen = (indices[..., None] == jnp.arange(psf_taps.shape[0], dtype=jnp.int32)).astype(jnp.float32)
    kernels = jnp.einsum("vek,kt->vet", chosen, psf_taps, precision=precise)
    return kernels / jnp.sum(kernels, axis=-1, keepdims=True)


def places(count, start):
    return jnp.arange(count, dtype=jnp.int32) + start


def banded(kernels, out_pos, in_pos):
    radius = (kernels.shape[-1] - 1) // 2
    offsets = in_pos[None, :] - out_pos[:, None] + radius
    selector = (offsets[:, :, None] == jnp.arange(kernels.shape[-1], dtype=jnp.int32)).astype(jnp.float32)
    return jnp.einsum("oit,vt->voi", selector, kernels, precision=precise)


def brick_kernels(psf_taps, kernel_index, brick_x, brick_y):
    anchor = jnp.zeros((), jnp.int32)
    views = kernel_index.shape[2]
    picked = lax.dynamic_slice(kernel_index, (brick_x, brick_y, anchor, anchor), (1, 1, views, 3))[0, 0]
    return lookup(psf_taps, picked)


def operators(kernels, planes, extent_x, extent_y):
    radius = (kernels.shape[-1] - 1) // 2
    along_z = banded(kernels[:, 2], places(planes, 0), places(planes, 0))
    along_x = banded(kernels[:, 0], places(extent_x + 2 * radius, -radius), places(extent_x, 0))
    along_y = banded(kernels[:, 1], places(extent_y + 2 * radius, -radius), places(extent_y, 0))
    return along_z, along_x, along_y


def forward_blur(inside, along_z, along_x, along_y):
    blurred = jnp.einsum("vpz,zxy->vpxy", along_z, inside, precision=precise)
    blurred = jnp.einsum("vix,vpxy->vpiy", along_x, blurred, precision=precise)
    return jnp.einsum("vjy,vpiy->vpij", along_y, blurred, precision=precise)


def adjoint_blur(spread, along_z, along_x, along_y):
    folded = jnp.einsum("vjy,vpij->vpiy", along_y, spread, precision=precise)
    folded = jnp.einsum("vix,vpiy->vpxy", along_x, folded, precision=precise)
    return jnp.einsum("vpz,vpxy->zxy", along_z, folded, precision=precise)


def reference(estimate, stored, placement, psf_taps, kernel_index):
    radius = (TAPS - 1) // 2
    bricks = N_GX * N_GY
    arranged = jnp.zeros_like(stored).at[placement].set(stored)
    measured = arranged.reshape(N_GX, N_GY, V, NZ, BX, BY).transpose(2, 3, 0, 4, 1, 5).reshape(V, NZ, NX, NY).astype(jnp.float32)
    anchor = jnp.zeros((), jnp.int32)

    def setup(brick_id):
        brick_id = jnp.asarray(brick_id).astype(jnp.int32)
        brick_x = brick_id // N_GY
        brick_y = brick_id % N_GY
        kernels = brick_kernels(psf_taps, kernel_index, brick_x, brick_y)
        return brick_x * BX, brick_y * BY, operators(kernels, NZ, BX, BY)

    current = estimate
    for iteration in range(ITERS):
        def spread_one(brick_id, summed):
            start_x, start_y, mats = setup(brick_id)
            inside = lax.dynamic_slice(current, (anchor, start_x, start_y), (NZ, BX, BY))
            spread = forward_blur(inside, mats[0], mats[1], mats[2])
            corner = (anchor, anchor, start_x, start_y)
            return lax.dynamic_update_slice(summed, lax.dynamic_slice(summed, corner, spread.shape) + spread, corner)

        summed = lax.fori_loop(0, bricks, spread_one, jnp.zeros((V, NZ, NX + 2 * radius, NY + 2 * radius), jnp.float32))
        blurred = summed[:, :, radius:radius + NX, radius:radius + NY]
        quotient = measured / blurred
        padded = jnp.pad(quotient, ((0, 0), (0, 0), (radius, radius), (radius, radius)))

        def fold_one(brick_id, correction):
            start_x, start_y, mats = setup(brick_id)
            spread = lax.dynamic_slice(padded, (anchor, anchor, start_x, start_y), (V, NZ, BX + 2 * radius, BY + 2 * radius))
            piece_corr = adjoint_blur(spread, mats[0], mats[1], mats[2]) / V
            return lax.dynamic_update_slice(correction, piece_corr, (anchor, start_x, start_y))

        correction = lax.fori_loop(0, bricks, fold_one, jnp.zeros_like(current))
        current = current * correction
    return current
```

```python
import functools

import jax
import jax.numpy as jnp
from jax import lax
from jax.experimental import pallas as pl
from jax.experimental.pallas import tpu as pltpu
from jax.sharding import PartitionSpec as P

ITERS = 2
MESH = pl.DeviceIdType.MESH
F32 = jnp.float32
BF16 = jnp.bfloat16


def dot(a, b):
    return jnp.dot(a, b, preferred_element_type=F32)


def dot_nt(a, b):
    return lax.dot_general(a, b, (((1,), (1,)), ((), ())), preferred_element_type=F32)


def iota(shape, dim):
    return lax.broadcasted_iota(jnp.int32, shape, dim)


def deblur_kernel(
    devices_x, devices_y, planes, ext_x, views,
    est_ref, arrived_ref, rows_ref, kidx_ref, psf_ref, out_ref,
    table, kz_small, kx_small, kz_wide, kx_wide, wy, kf, kt,
    cur, cbuf, zcat, blur, rim, rim_send, rim_recv, qext, q_send, q_recv, u, part, part_recv, meas,
    send_sem, recv_sem,
):
    zx = planes * ext_x
    ny = est_ref.shape[1]
    taps = psf_ref.shape[1]
    rad = (taps - 1) // 2
    half = zx // 2
    gx = lax.axis_index("gx")
    gy = lax.axis_index("gy")
    has = {
        "left": gx > 0,
        "right": gx < devices_x - 1,
        "down": gy > 0,
        "up": gy < devices_y - 1,
    }
    to = {
        "left": (gx - 1, gy),
        "right": (gx + 1, gy),
        "down": (gx, gy - 1),
        "up": (gx, gy + 1),
    }
    slot_of = {"left": 0, "right": 1, "down": 0, "up": 1}
    back = {"left": "right", "right": "left", "down": "up", "up": "down"}

    barrier = pltpu.get_barrier_semaphore()
    for side in has:
        @pl.when(has[side])
        def _(side=side):
            pl.semaphore_signal(barrier, inc=1, device_id=to[side], device_id_type=MESH)

    def send(side, kind, src, dst):
        num = kind * 2 + slot_of[side]

        @pl.when(has[side])
        def _():
            pltpu.make_async_remote_copy(
                src_ref=src, dst_ref=dst, send_sem=send_sem.at[num],
                recv_sem=recv_sem.at[kind * 2 + slot_of[side]],
                device_id=to[side], device_id_type=MESH,
            ).start()

    def wait_send(side, kind, src):
        num = kind * 2 + slot_of[side]

        @pl.when(has[side])
        def _():
            pltpu.make_async_remote_copy(
                src_ref=src, dst_ref=src, send_sem=send_sem.at[num], recv_sem=recv_sem.at[num],
                device_id=to[side], device_id_type=MESH,
            ).wait_send()

    def wait_recv(side, kind, dst):
        num = kind * 2 + slot_of[back[side]]

        @pl.when(has[side])
        def _():
            pltpu.make_async_remote_copy(
                src_ref=dst, dst_ref=dst, send_sem=send_sem.at[num], recv_sem=recv_sem.at[num],
                device_id=to[side], device_id_type=MESH,
            ).wait_recv()

    def clear_missing(side, dst):
        @pl.when(jnp.logical_not(has[side]))
        def _():
            dst[...] = jnp.zeros(dst.shape, dst.dtype)

    cur[...] = est_ref[...]
    cbuf[0, 1] = cur[...].astype(BF16)
    for it in range(ITERS):
        clear_missing("left", cbuf.at[it, 0])
        clear_missing("right", cbuf.at[it, 2])
        for kind_buf in (rim_recv, q_recv):
            clear_missing("down", kind_buf.at[it, 0])
            clear_missing("up", kind_buf.at[it, 1])
        clear_missing("left", part_recv.at[it, 0])
        clear_missing("right", part_recv.at[it, 1])
    peers = sum(present.astype(jnp.int32) for present in has.values())
    pl.semaphore_wait(barrier, peers)

    def send_current(it):
        send("left", 4 * it, cbuf.at[it, 1], cbuf.at[it, 2])
        send("right", 4 * it, cbuf.at[it, 1], cbuf.at[it, 0])

    send_current(0)

    weights = psf_ref[...]
    weights = weights / jnp.sum(weights, axis=1, keepdims=True)
    tap = iota((taps, 128), 0)
    lane = iota((taps, 128), 1)

    def spread_taps(distance):
        select = (lane == jnp.where(distance < 0, distance + 128, distance)).astype(F32)
        return jnp.dot(weights, select, precision=lax.Precision.HIGHEST, preferred_element_type=F32)

    blocks = [tap - rad, rad - tap]
    blocks += [tap - rad - o for o in (-ext_x, 0, ext_x)]
    blocks += [rad + o - tap for o in (-ext_x, 0, ext_x)]
    for num, distance in enumerate(blocks):
        table[num] = spread_taps(distance)
    rounded = table[1].astype(BF16).astype(F32)
    scale = 1.0 / jnp.sum(rounded, axis=1, keepdims=True)
    table[8] = jnp.broadcast_to(scale, (scale.shape[0], 128))

    def toeplitz(base, count):
        return pltpu.roll(jnp.broadcast_to(base, (count, 128)), 0, 1, stride=1, stride_axis=0)

    def two_parts(matrix, width):
        where = iota(matrix.shape, 1)
        low = matrix - matrix.astype(BF16).astype(F32)
        return jnp.where(where < width, matrix, pltpu.roll(low, width, 1)).astype(BF16)

    for i in range(3):
        brick_x = jnp.clip(gx + (i - 1), 0, devices_x - 1)
        for v in range(views):
            n = i * views + v
            first = ((brick_x * devices_y + gy) * views + v) * 3
            id_x, id_y, id_z = (kidx_ref[first + e] for e in range(3))
            factor = table[8, pl.ds(id_y, 1), :]
            for way in range(2):
                base = table[way, pl.ds(id_z, 1), :] * factor
                at = (way * 3 * views + n) * planes
                kz_small[at:at + planes, :] = two_parts(toeplitz(base, planes), planes)
                block = 2 + 3 * way + i
                base = table[block, pl.ds(id_x, 1), :]
                at = (way * 3 * views + n) * ext_x
                kx_small[at:at + ext_x, :] = two_parts(toeplitz(base, ext_x), ext_x)
            ring = toeplitz(table[1, pl.ds(id_y, 1), :], ny)
            apart = iota((ny, 128), 1) - iota((ny, 128), 0)
            near = (apart >= -rad) & (apart <= rad)
            wy[v, i * ny:(i + 1) * ny, 0:128] = jnp.where(near, ring, 0.0).astype(BF16)
            edge = jnp.where(near, 0.0, ring)
            if v:
                edge = pltpu.roll(edge, 32 * v, 1)
            wy[v, i * ny:(i + 1) * ny, 128:256] = edge.astype(BF16)

    wide = (128, zx)
    row = iota(wide, 0)
    col = iota(wide, 1)
    col_z = col // ext_x
    col_x = lax.rem(col, ext_x)
    pick_z = ((row == col_z) | (row == col_z + planes)).astype(F32).astype(BF16)
    pick_x = ((row == col_x) | (row == col_x + ext_x)).astype(F32).astype(BF16)

    def expand(n, carry):
        at = pl.multiple_of(n * 96, 32)
        res = dot(kz_small[pl.ds(at, 96), :], pick_z)
        for part_num in range(zx // 128):
            kz_wide[part_num, pl.ds(at, 96), :] = res[:, part_num * 128:(part_num + 1) * 128]
        return carry

    lax.fori_loop(0, kz_small.shape[0] // 96, expand, 0)
    kx_wide[...] = dot(kx_small[...], pick_x[:, 0:128])

    def build(way):
        def one(n, carry):
            i = n // views
            v = lax.rem(n, views)
            num = way * 3 * views + n
            tile = kx_wide[pl.ds(pl.multiple_of(num * ext_x, 16), ext_x), :]
            for z in range(planes):
                for b in range(zx // 128):
                    line = kz_wide[b, pl.ds(num * planes + z, 1), :]
                    value = (jnp.broadcast_to(line, (ext_x, 128)) * tile).astype(BF16)
                    if way == 0:
                        at = pl.multiple_of(v * zx + z * ext_x, 16)
                        kf[i, pl.ds(at, ext_x), b * 128:(b + 1) * 128] = value
                    else:
                        at = pl.multiple_of(v * zx + b * 128, 128)
                        kt[i, z * ext_x:(z + 1) * ext_x, pl.ds(at, 128)] = value
            return carry

        lax.fori_loop(0, 3 * views, one, 0)

    build(0)

    lane_half = iota((half, 128), 1)
    low_half = lax.rem(lane_half, 32) < 16

    def fold(value, first):
        top, bottom = value[0:half], value[half:zx]
        if first:
            return jnp.where(low_half, top, pltpu.roll(bottom, 16, 1)).astype(BF16)
        return jnp.where(low_half, pltpu.roll(bottom, 112, 1), top).astype(BF16)

    def unfold(from_first, from_second):
        a, b = from_first.astype(F32), from_second.astype(F32)
        top = jnp.where(low_half, a, b)
        bottom = jnp.where(low_half, pltpu.roll(a, 112, 1), pltpu.roll(b, 16, 1))
        return top, bottom

    def forward_zx(it, i):
        def one(v, carry):
            at = pl.multiple_of(v * zx, zx)
            zcat[pl.ds(at, zx), i * ny:(i + 1) * ny] = dot(
                kf[i, pl.ds(at, zx), :], cbuf[it, i]
            ).astype(BF16)
            return carry

        lax.fori_loop(0, views, one, 0)

    def forward_y():
        rim[...] = jnp.zeros(rim.shape, F32)

        def one(v, carry):
            at = pl.multiple_of(v * zx, zx)
            res = dot(zcat[pl.ds(at, zx), :], wy[v])
            blur[pl.ds(at, zx), :] = res[:, 0:128]
            rim[...] += res[:, 128:256]
            return carry

        lax.fori_loop(0, views, one, 0)

    def adjoint_y():
        def one(v, carry):
            at = pl.multiple_of(v * zx, zx)
            res = dot_nt(qext[pl.ds(at, zx), :], wy[v]).astype(BF16)
            for i in range(3):
                u[i, pl.ds(at, zx), :] = res[:, i * ny:(i + 1) * ny]
            return carry

        lax.fori_loop(0, views, one, 0)

    lane_q = iota((zx, 128), 1)
    low_q = lax.rem(lane_q, 32) < 16

    for it in range(ITERS):
        kind_c, kind_rim, kind_q, kind_p = (4 * it + k for k in range(4))
        forward_zx(it, 1)
        wait_recv("left", kind_c, cbuf.at[it, 0])
        wait_recv("right", kind_c, cbuf.at[it, 2])
        forward_zx(it, 0)
        forward_zx(it, 2)
        forward_y()
        rim_send[it, 1] = fold(rim[...], True)
        rim_send[it, 0] = fold(rim[...], False)
        send("up", kind_rim, rim_send.at[it, 1], rim_recv.at[it, 0])
        send("down", kind_rim, rim_send.at[it, 0], rim_recv.at[it, 1])
        if it == 0:
            build(1)

            def take(p, carry):
                meas[pl.ds(pl.multiple_of(p * ext_x, ext_x), ext_x), :] = arrived_ref[rows_ref[p]]
                return carry

            lax.fori_loop(0, views * planes, take, 0)
        wait_recv("down", kind_rim, rim_recv.at[it, 0])
        wait_recv("up", kind_rim, rim_recv.at[it, 1])
        tops = unfold(rim_recv[it, 0], rim_recv[it, 1])
        rim[0:half] = tops[0]
        rim[half:zx] = tops[1]
        packed = jnp.zeros((zx, 128), F32)
        for v in range(views):
            add = rim[...]
            if v:
                add = pltpu.roll(add, 128 - 32 * v, 1)
            edge = (lane_q < rad) | (lane_q >= 128 - rad)
            total = blur[v * zx:(v + 1) * zx, :] + jnp.where(edge, add, 0.0)
            q = meas[v * zx:(v + 1) * zx, :].astype(F32) / total
            qext[v * zx:(v + 1) * zx, 0:128] = q.astype(BF16)
            moved = pltpu.roll(q, 32 * v, 1) if v else q
            place = lax.rem(lane_q - 32 * v + 128 + rad, 128)
            packed = jnp.where(place < 2 * rad, moved, packed)
        q_send[it, 0] = fold(packed, True)
        q_send[it, 1] = fold(packed, False)
        send("down", kind_q, q_send.at[it, 0], q_recv.at[it, 1])
        send("up", kind_q, q_send.at[it, 1], q_recv.at[it, 0])
        wait_recv("down", kind_q, q_recv.at[it, 0])
        wait_recv("up", kind_q, q_recv.at[it, 1])
        tops = unfold(q_recv[it, 1], q_recv[it, 0])
        for v in range(views):
            qext[v * zx:v * zx + half, 128:256] = tops[0].astype(BF16)
            qext[v * zx + half:(v + 1) * zx, 128:256] = tops[1].astype(BF16)
        adjoint_y()
        part[it, 0] = dot(kt[0], u[0])
        send("left", kind_p, part.at[it, 0], part_recv.at[it, 1])
        part[it, 1] = dot(kt[2], u[2])
        send("right", kind_p, part.at[it, 1], part_recv.at[it, 0])
        own = dot(kt[1], u[1])
        wait_recv("left", kind_p, part_recv.at[it, 0])
        wait_recv("right", kind_p, part_recv.at[it, 1])
        correction = (own + part_recv[it, 0] + part_recv[it, 1]) * (1.0 / views)
        updated = cur[...] * correction
        if it < ITERS - 1:
            cur[...] = updated
            cbuf[it + 1, 1] = updated.astype(BF16)
            send_current(it + 1)
        else:
            out_ref[...] = updated

    for it in range(ITERS):
        kind_c, kind_rim, kind_q, kind_p = (4 * it + k for k in range(4))
        for side in ("left", "right"):
            wait_send(side, kind_c, cbuf.at[it, 1])
            wait_send(side, kind_p, part.at[it, 0])
        for side in ("down", "up"):
            wait_send(side, kind_rim, rim_send.at[it, 0])
            wait_send(side, kind_q, q_send.at[it, 0])


def exchange(stored, placement, devices):
    slots = stored.shape[0]
    me = lax.axis_index("gx") * lax.axis_size("gy") + lax.axis_index("gy")
    slot = jnp.arange(slots, dtype=jnp.int32)[None, :]
    own = lax.dynamic_slice_in_dim(placement, me * slots, slots) // slots
    match = own[None, :] == jnp.arange(devices, dtype=jnp.int32)[:, None]
    first = jnp.min(jnp.where(match, slot, slots - 1), axis=1)
    last = jnp.max(jnp.where(match, slot, 0), axis=1)
    source = jnp.stack([first, last], axis=1).reshape(-1)
    outgoing = jnp.take(stored, source, axis=0, mode="clip")
    outgoing = outgoing.reshape((devices, 2) + stored.shape[1:])
    arrived = lax.all_to_all(outgoing, ("gx", "gy"), split_axis=0, concat_axis=0, tiled=True)
    everything = placement.reshape(devices, slots)
    wanted = everything // slots == me
    item = everything % slots
    first = jnp.min(jnp.where(wanted, slot, slots), axis=1, keepdims=True)
    last = jnp.max(jnp.where(wanted, slot, -1), axis=1, keepdims=True)
    item_first = jnp.max(jnp.where(slot == first, item, -1), axis=1)
    item_last = jnp.max(jnp.where((slot == last) & (last > first), item, -1), axis=1)
    items = jnp.arange(slots, dtype=jnp.int32)[:, None]
    origin = jnp.arange(devices, dtype=jnp.int32)[None, :]
    row = jnp.max(
        jnp.where(item_first[None, :] == items, 2 * origin, 0)
        + jnp.where(item_last[None, :] == items, 2 * origin + 1, 0),
        axis=1,
    )
    return arrived.reshape((2 * devices,) + stored.shape[1:]), row


def solution(mesh):
    devices_x, devices_y = mesh.shape["gx"], mesh.shape["gy"]

    def shards(estimate, stored, placement, psf_taps, kernel_index):
        planes, ext_x, ny = estimate.shape
        zx = planes * ext_x
        views = kernel_index.shape[2]
        arrived, row = exchange(stored, placement, devices_x * devices_y)
        vmem = pl.BlockSpec(memory_space=pltpu.VMEM)
        smem = pl.BlockSpec(memory_space=pltpu.SMEM)
        n = 3 * views
        half = zx // 2
        refined = pl.pallas_call(
            functools.partial(deblur_kernel, devices_x, devices_y, planes, ext_x, views),
            out_shape=jax.ShapeDtypeStruct((zx, ny), F32),
            in_specs=[vmem, vmem, smem, smem, vmem],
            out_specs=vmem,
            scratch_shapes=[
                pltpu.VMEM((9, psf_taps.shape[0], 128), F32),
                pltpu.VMEM((2 * n * planes, 128), BF16),
                pltpu.VMEM((2 * n * ext_x, 128), BF16),
                pltpu.VMEM((zx // 128, 2 * n * planes, 128), F32),
                pltpu.VMEM((2 * n * ext_x, 128), F32),
                pltpu.VMEM((views, 3 * ny, 256), BF16),
                pltpu.VMEM((3, views * zx, zx), BF16),
                pltpu.VMEM((3, zx, views * zx), BF16),
                pltpu.VMEM((zx, ny), F32),
                pltpu.VMEM((ITERS, 3, zx, ny), BF16),
                pltpu.VMEM((views * zx, 3 * ny), BF16),
                pltpu.VMEM((views * zx, ny), F32),
                pltpu.VMEM((zx, 128), F32),
                pltpu.VMEM((ITERS, 2, half, 128), BF16),
                pltpu.VMEM((ITERS, 2, half, 128), BF16),
                pltpu.VMEM((views * zx, 256), BF16),
                pltpu.VMEM((ITERS, 2, half, 128), BF16),
                pltpu.VMEM((ITERS, 2, half, 128), BF16),
                pltpu.VMEM((3, views * zx, ny), BF16),
                pltpu.VMEM((ITERS, 2, zx, ny), F32),
                pltpu.VMEM((ITERS, 2, zx, ny), F32),
                pltpu.VMEM((views * zx, ny), BF16),
                pltpu.SemaphoreType.DMA((8 * ITERS,)),
                pltpu.SemaphoreType.DMA((8 * ITERS,)),
            ],
            compiler_params=pltpu.CompilerParams(
                collective_id=0, has_side_effects=True, vmem_limit_bytes=60 * 1024 * 1024
            ),
        )(
            estimate.reshape(zx, ny),
            arrived,
            row,
            kernel_index.reshape(-1),
            psf_taps,
        )
        return refined.reshape(planes, ext_x, ny)

    return jax.shard_map(
        shards,
        mesh=mesh,
        in_specs=(P(None, "gx", "gy"), P(("gx", "gy"), None, None), P(), P(), P()),
        out_specs=P(None, "gx", "gy"),
        check_vma=False,
    )
```

```python
import functools

import jax
import jax.numpy as jnp
from jax import lax
from jax.experimental import pallas as pl
from jax.experimental.pallas import tpu as pltpu
from jax.sharding import PartitionSpec as P

ITERS = 2
MESH = pl.DeviceIdType.MESH
F32 = jnp.float32
BF16 = jnp.bfloat16


def dot(a, b):
    return jnp.dot(a, b, preferred_element_type=F32)


def dot_nt(a, b):
    return lax.dot_general(a, b, (((1,), (1,)), ((), ())), preferred_element_type=F32)


def iota(shape, dim):
    return lax.broadcasted_iota(jnp.int32, shape, dim)


def deblur_kernel(
    devices_x, devices_y, planes, ext_x, views,
    est_ref, planes_ref, rows_ref, kidx_ref, psf_ref, out_ref,
    table, kz_small, kx_small, kz_wide, kx_wide, wy, kf, kt,
    cur, cbuf, zcat, blur, rim, rim_send, rim_recv, qext, q_send, q_recv, u, part, part_recv, meas, arrived,
    send_sem, recv_sem, plane_send_sem, plane_recv_sem,
):
    zx = planes * ext_x
    ny = est_ref.shape[1]
    taps = psf_ref.shape[1]
    rad = (taps - 1) // 2
    half = zx // 2
    gx = lax.axis_index("gx")
    gy = lax.axis_index("gy")
    has = {
        "left": gx > 0,
        "right": gx < devices_x - 1,
        "down": gy > 0,
        "up": gy < devices_y - 1,
    }
    to = {
        "left": (gx - 1, gy),
        "right": (gx + 1, gy),
        "down": (gx, gy - 1),
        "up": (gx, gy + 1),
    }
    slot_of = {"left": 0, "right": 1, "down": 0, "up": 1}
    back = {"left": "right", "right": "left", "down": "up", "up": "down"}

    devices = devices_x * devices_y
    me = gx * devices_y + gy

    def partner(k):
        other = lax.rem(me + k, devices)
        return other, (other // devices_y, lax.rem(other, devices_y))

    barrier = pltpu.get_barrier_semaphore()

    def greet(k, carry):
        pl.semaphore_signal(barrier, inc=1, device_id=partner(k)[1], device_id_type=MESH)
        return carry

    lax.fori_loop(1, devices, greet, 0)

    def send(side, kind, src, dst):
        num = kind * 2 + slot_of[side]

        @pl.when(has[side])
        def _():
            pltpu.make_async_remote_copy(
                src_ref=src, dst_ref=dst, send_sem=send_sem.at[num],
                recv_sem=recv_sem.at[kind * 2 + slot_of[side]],
                device_id=to[side], device_id_type=MESH,
            ).start()

    def wait_send(side, kind, src):
        num = kind * 2 + slot_of[side]

        @pl.when(has[side])
        def _():
            pltpu.make_async_remote_copy(
                src_ref=src, dst_ref=src, send_sem=send_sem.at[num], recv_sem=recv_sem.at[num],
                device_id=to[side], device_id_type=MESH,
            ).wait_send()

    def wait_recv(side, kind, dst):
        num = kind * 2 + slot_of[back[side]]

        @pl.when(has[side])
        def _():
            pltpu.make_async_remote_copy(
                src_ref=dst, dst_ref=dst, send_sem=send_sem.at[num], recv_sem=recv_sem.at[num],
                device_id=to[side], device_id_type=MESH,
            ).wait_recv()

    def clear_missing(side, dst):
        @pl.when(jnp.logical_not(has[side]))
        def _():
            dst[...] = jnp.zeros(dst.shape, dst.dtype)

    cur[...] = est_ref[...]
    cbuf[0, 1] = cur[...].astype(BF16)
    for it in range(ITERS):
        clear_missing("left", cbuf.at[it, 0])
        clear_missing("right", cbuf.at[it, 2])
        for kind_buf in (rim_recv, q_recv):
            clear_missing("down", kind_buf.at[it, 0])
            clear_missing("up", kind_buf.at[it, 1])
        clear_missing("left", part_recv.at[it, 0])
        clear_missing("right", part_recv.at[it, 1])

    def send_current(it):
        send("left", 4 * it, cbuf.at[it, 1], cbuf.at[it, 2])
        send("right", 4 * it, cbuf.at[it, 1], cbuf.at[it, 0])

    def send_planes(k, carry):
        other, where = partner(k)
        pltpu.make_async_remote_copy(
            src_ref=planes_ref.at[other], dst_ref=arrived.at[k],
            send_sem=plane_send_sem, recv_sem=plane_recv_sem,
            device_id=where, device_id_type=MESH,
        ).start()
        return carry

    def all_planes():
        return pltpu.make_async_remote_copy(
            src_ref=arrived.at[pl.ds(1, devices - 1)], dst_ref=arrived.at[pl.ds(1, devices - 1)],
            send_sem=plane_send_sem, recv_sem=plane_recv_sem,
            device_id=partner(1)[1], device_id_type=MESH,
        )

    weights = psf_ref[...]
    weights = weights / jnp.sum(weights, axis=1, keepdims=True)
    tap = iota((taps, 128), 0)
    lane = iota((taps, 128), 1)

    def spread_taps(distance):
        select = (lane == jnp.where(distance < 0, distance + 128, distance)).astype(F32)
        return jnp.dot(weights, select, precision=lax.Precision.HIGHEST, preferred_element_type=F32)

    blocks = [tap - rad, rad - tap]
    blocks += [tap - rad - o for o in (-ext_x, 0, ext_x)]
    blocks += [rad + o - tap for o in (-ext_x, 0, ext_x)]
    for num, distance in enumerate(blocks):
        table[num] = spread_taps(distance)
    rounded = table[1].astype(BF16).astype(F32)
    scale = 1.0 / jnp.sum(rounded, axis=1, keepdims=True)
    table[8] = jnp.broadcast_to(scale, (scale.shape[0], 128))

    def toeplitz(base, count):
        return pltpu.roll(jnp.broadcast_to(base, (count, 128)), 0, 1, stride=1, stride_axis=0)

    def two_parts(matrix, width):
        where = iota(matrix.shape, 1)
        low = matrix - matrix.astype(BF16).astype(F32)
        return jnp.where(where < width, matrix, pltpu.roll(low, width, 1)).astype(BF16)

    for i in range(3):
        brick_x = jnp.clip(gx + (i - 1), 0, devices_x - 1)
        for v in range(views):
            n = i * views + v
            first = ((brick_x * devices_y + gy) * views + v) * 3
            id_x, id_y, id_z = (kidx_ref[first + e] for e in range(3))
            factor = table[8, pl.ds(id_y, 1), :]
            for way in range(2):
                base = table[way, pl.ds(id_z, 1), :] * factor
                at = (way * 3 * views + n) * planes
                kz_small[at:at + planes, :] = two_parts(toeplitz(base, planes), planes)
                block = 2 + 3 * way + i
                base = table[block, pl.ds(id_x, 1), :]
                at = (way * 3 * views + n) * ext_x
                kx_small[at:at + ext_x, :] = two_parts(toeplitz(base, ext_x), ext_x)
            ring = toeplitz(table[1, pl.ds(id_y, 1), :], ny)
            apart = iota((ny, 128), 1) - iota((ny, 128), 0)
            near = (apart >= -rad) & (apart <= rad)
            wy[v, i * ny:(i + 1) * ny, 0:128] = jnp.where(near, ring, 0.0).astype(BF16)
            edge = jnp.where(near, 0.0, ring)
            if v:
                edge = pltpu.roll(edge, 32 * v, 1)
            wy[v, i * ny:(i + 1) * ny, 128:256] = edge.astype(BF16)

    pl.semaphore_wait(barrier, devices - 1)
    send_current(0)
    lax.fori_loop(1, devices, send_planes, 0)
    arrived[0] = planes_ref[me]

    wide = (128, zx)
    row = iota(wide, 0)
    col = iota(wide, 1)
    col_z = col // ext_x
    col_x = lax.rem(col, ext_x)
    pick_z = ((row == col_z) | (row == col_z + planes)).astype(F32).astype(BF16)
    pick_x = ((row == col_x) | (row == col_x + ext_x)).astype(F32).astype(BF16)

    def expand(n, carry):
        at = pl.multiple_of(n * 96, 32)
        res = dot(kz_small[pl.ds(at, 96), :], pick_z)
        for part_num in range(zx // 128):
            kz_wide[part_num, pl.ds(at, 96), :] = res[:, part_num * 128:(part_num + 1) * 128]
        return carry

    lax.fori_loop(0, kz_small.shape[0] // 96, expand, 0)
    kx_wide[...] = dot(kx_small[...], pick_x[:, 0:128])

    def build(way):
        def one(n, carry):
            i = n // views
            v = lax.rem(n, views)
            num = way * 3 * views + n
            tile = kx_wide[pl.ds(pl.multiple_of(num * ext_x, 16), ext_x), :]
            for z in range(planes):
                for b in range(zx // 128):
                    line = kz_wide[b, pl.ds(num * planes + z, 1), :]
                    value = (jnp.broadcast_to(line, (ext_x, 128)) * tile).astype(BF16)
                    if way == 0:
                        at = pl.multiple_of(v * zx + z * ext_x, 16)
                        kf[i, pl.ds(at, ext_x), b * 128:(b + 1) * 128] = value
                    else:
                        at = pl.multiple_of(v * zx + b * 128, 128)
                        kt[i, z * ext_x:(z + 1) * ext_x, pl.ds(at, 128)] = value
            return carry

        lax.fori_loop(0, 3 * views, one, 0)

    build(0)

    lane_half = iota((half, 128), 1)
    low_half = lax.rem(lane_half, 32) < 16

    def fold(value, first):
        top, bottom = value[0:half], value[half:zx]
        if first:
            return jnp.where(low_half, top, pltpu.roll(bottom, 16, 1)).astype(BF16)
        return jnp.where(low_half, pltpu.roll(bottom, 112, 1), top).astype(BF16)

    def unfold(from_first, from_second):
        a, b = from_first.astype(F32), from_second.astype(F32)
        top = jnp.where(low_half, a, b)
        bottom = jnp.where(low_half, pltpu.roll(a, 112, 1), pltpu.roll(b, 16, 1))
        return top, bottom

    def forward_zx(it, i):
        def one(v, carry):
            at = pl.multiple_of(v * zx, zx)
            zcat[pl.ds(at, zx), i * ny:(i + 1) * ny] = dot(
                kf[i, pl.ds(at, zx), :], cbuf[it, i]
            ).astype(BF16)
            return carry

        lax.fori_loop(0, views, one, 0)

    def forward_y():
        rim[...] = jnp.zeros(rim.shape, F32)

        def one(v, carry):
            at = pl.multiple_of(v * zx, zx)
            res = dot(zcat[pl.ds(at, zx), :], wy[v])
            blur[pl.ds(at, zx), :] = res[:, 0:128]
            rim[...] += res[:, 128:256]
            return carry

        lax.fori_loop(0, views, one, 0)

    def adjoint_y():
        def one(v, carry):
            at = pl.multiple_of(v * zx, zx)
            res = dot_nt(qext[pl.ds(at, zx), :], wy[v]).astype(BF16)
            for i in range(3):
                u[i, pl.ds(at, zx), :] = res[:, i * ny:(i + 1) * ny]
            return carry

        lax.fori_loop(0, views, one, 0)

    lane_q = iota((zx, 128), 1)
    low_q = lax.rem(lane_q, 32) < 16

    for it in range(ITERS):
        kind_c, kind_rim, kind_q, kind_p = (4 * it + k for k in range(4))
        forward_zx(it, 1)
        wait_recv("left", kind_c, cbuf.at[it, 0])
        wait_recv("right", kind_c, cbuf.at[it, 2])
        forward_zx(it, 0)
        forward_zx(it, 2)
        forward_y()
        rim_send[it, 1] = fold(rim[...], True)
        rim_send[it, 0] = fold(rim[...], False)
        send("up", kind_rim, rim_send.at[it, 1], rim_recv.at[it, 0])
        send("down", kind_rim, rim_send.at[it, 0], rim_recv.at[it, 1])
        if it == 0:
            build(1)

            all_planes().wait_recv()

            def take(p, carry):
                place = rows_ref[p]
                at = pl.ds(pl.multiple_of(p * ext_x, ext_x), ext_x)
                meas[at, :] = arrived[place // 2, lax.rem(place, 2)]
                return carry

            lax.fori_loop(0, views * planes, take, 0)
        wait_recv("down", kind_rim, rim_recv.at[it, 0])
        wait_recv("up", kind_rim, rim_recv.at[it, 1])
        tops = unfold(rim_recv[it, 0], rim_recv[it, 1])
        rim[0:half] = tops[0]
        rim[half:zx] = tops[1]
        packed = jnp.zeros((zx, 128), F32)
        for v in range(views):
            add = rim[...]
            if v:
                add = pltpu.roll(add, 128 - 32 * v, 1)
            edge = (lane_q < rad) | (lane_q >= 128 - rad)
            total = blur[v * zx:(v + 1) * zx, :] + jnp.where(edge, add, 0.0)
            q = meas[v * zx:(v + 1) * zx, :].astype(F32) / total
            qext[v * zx:(v + 1) * zx, 0:128] = q.astype(BF16)
            moved = pltpu.roll(q, 32 * v, 1) if v else q
            place = lax.rem(lane_q - 32 * v + 128 + rad, 128)
            packed = jnp.where(place < 2 * rad, moved, packed)
        q_send[it, 0] = fold(packed, True)
        q_send[it, 1] = fold(packed, False)
        send("down", kind_q, q_send.at[it, 0], q_recv.at[it, 1])
        send("up", kind_q, q_send.at[it, 1], q_recv.at[it, 0])
        wait_recv("down", kind_q, q_recv.at[it, 0])
        wait_recv("up", kind_q, q_recv.at[it, 1])
        tops = unfold(q_recv[it, 1], q_recv[it, 0])
        for v in range(views):
            qext[v * zx:v * zx + half, 128:256] = tops[0].astype(BF16)
            qext[v * zx + half:(v + 1) * zx, 128:256] = tops[1].astype(BF16)
        adjoint_y()
        part[it, 0] = dot(kt[0], u[0])
        send("left", kind_p, part.at[it, 0], part_recv.at[it, 1])
        part[it, 1] = dot(kt[2], u[2])
        send("right", kind_p, part.at[it, 1], part_recv.at[it, 0])
        own = dot(kt[1], u[1])
        wait_recv("left", kind_p, part_recv.at[it, 0])
        wait_recv("right", kind_p, part_recv.at[it, 1])
        correction = (own + part_recv[it, 0] + part_recv[it, 1]) * (1.0 / views)
        updated = cur[...] * correction
        if it < ITERS - 1:
            cur[...] = updated
            cbuf[it + 1, 1] = updated.astype(BF16)
            send_current(it + 1)
        else:
            out_ref[...] = updated

    all_planes().wait_send()
    for it in range(ITERS):
        kind_c, kind_rim, kind_q, kind_p = (4 * it + k for k in range(4))
        for side in ("left", "right"):
            wait_send(side, kind_c, cbuf.at[it, 1])
            wait_send(side, kind_p, part.at[it, 0])
        for side in ("down", "up"):
            wait_send(side, kind_rim, rim_send.at[it, 0])
            wait_send(side, kind_q, q_send.at[it, 0])


def exchange(stored, placement, devices):
    slots = stored.shape[0]
    me = lax.axis_index("gx") * lax.axis_size("gy") + lax.axis_index("gy")
    slot = jnp.arange(slots, dtype=jnp.int32)[None, :]
    own = lax.dynamic_slice_in_dim(placement, me * slots, slots) // slots
    match = own[None, :] == jnp.arange(devices, dtype=jnp.int32)[:, None]
    first = jnp.min(jnp.where(match, slot, slots - 1), axis=1)
    last = jnp.max(jnp.where(match, slot, 0), axis=1)
    source = jnp.stack([first, last], axis=1).reshape(-1)
    outgoing = jnp.take(stored, source, axis=0, mode="clip")
    outgoing = outgoing.reshape((devices, 2) + stored.shape[1:])
    everything = placement.reshape(devices, slots)
    wanted = everything // slots == me
    item = everything % slots
    first = jnp.min(jnp.where(wanted, slot, slots), axis=1, keepdims=True)
    last = jnp.max(jnp.where(wanted, slot, -1), axis=1, keepdims=True)
    item_first = jnp.max(jnp.where(slot == first, item, -1), axis=1)
    item_last = jnp.max(jnp.where((slot == last) & (last > first), item, -1), axis=1)
    items = jnp.arange(slots, dtype=jnp.int32)[:, None]
    origin = (me - jnp.arange(devices, dtype=jnp.int32)[None, :]) % devices
    row = jnp.max(
        jnp.where(item_first[None, :] == items, 2 * origin, 0)
        + jnp.where(item_last[None, :] == items, 2 * origin + 1, 0),
        axis=1,
    )
    return outgoing, row


def solution(mesh):
    devices_x, devices_y = mesh.shape["gx"], mesh.shape["gy"]

    def shards(estimate, stored, placement, psf_taps, kernel_index):
        planes, ext_x, ny = estimate.shape
        zx = planes * ext_x
        views = kernel_index.shape[2]
        outgoing, row = exchange(stored, placement, devices_x * devices_y)
        vmem = pl.BlockSpec(memory_space=pltpu.VMEM)
        smem = pl.BlockSpec(memory_space=pltpu.SMEM)
        n = 3 * views
        half = zx // 2
        refined = pl.pallas_call(
            functools.partial(deblur_kernel, devices_x, devices_y, planes, ext_x, views),
            out_shape=jax.ShapeDtypeStruct((zx, ny), F32),
            in_specs=[vmem, vmem, smem, smem, vmem],
            out_specs=vmem,
            scratch_shapes=[
                pltpu.VMEM((9, psf_taps.shape[0], 128), F32),
                pltpu.VMEM((2 * n * planes, 128), BF16),
                pltpu.VMEM((2 * n * ext_x, 128), BF16),
                pltpu.VMEM((zx // 128, 2 * n * planes, 128), F32),
                pltpu.VMEM((2 * n * ext_x, 128), F32),
                pltpu.VMEM((views, 3 * ny, 256), BF16),
                pltpu.VMEM((3, views * zx, zx), BF16),
                pltpu.VMEM((3, zx, views * zx), BF16),
                pltpu.VMEM((zx, ny), F32),
                pltpu.VMEM((ITERS, 3, zx, ny), BF16),
                pltpu.VMEM((views * zx, 3 * ny), BF16),
                pltpu.VMEM((views * zx, ny), F32),
                pltpu.VMEM((zx, 128), F32),
                pltpu.VMEM((ITERS, 2, half, 128), BF16),
                pltpu.VMEM((ITERS, 2, half, 128), BF16),
                pltpu.VMEM((views * zx, 256), BF16),
                pltpu.VMEM((ITERS, 2, half, 128), BF16),
                pltpu.VMEM((ITERS, 2, half, 128), BF16),
                pltpu.VMEM((3, views * zx, ny), BF16),
                pltpu.VMEM((ITERS, 2, zx, ny), F32),
                pltpu.VMEM((ITERS, 2, zx, ny), F32),
                pltpu.VMEM((views * zx, ny), BF16),
                pltpu.VMEM(outgoing.shape, BF16),
                pltpu.SemaphoreType.DMA((8 * ITERS,)),
                pltpu.SemaphoreType.DMA((8 * ITERS,)),
                pltpu.SemaphoreType.DMA,
                pltpu.SemaphoreType.DMA,
            ],
            compiler_params=pltpu.CompilerParams(
                collective_id=0, has_side_effects=True, vmem_limit_bytes=60 * 1024 * 1024
            ),
        )(
            estimate.reshape(zx, ny),
            outgoing,
            row,
            kernel_index.reshape(-1),
            psf_taps,
        )
        return refined.reshape(planes, ext_x, ny)

    return jax.shard_map(
        shards,
        mesh=mesh,
        in_specs=(P(None, "gx", "gy"), P(("gx", "gy"), None, None), P(), P(), P()),
        out_specs=P(None, "gx", "gy"),
        check_vma=False,
    )
```

```python
import functools

import jax
import jax.numpy as jnp
from jax import lax
from jax.experimental import pallas as pl
from jax.experimental.pallas import tpu as pltpu
from jax.sharding import PartitionSpec as P

ITERS = 2
MESH = pl.DeviceIdType.MESH
F32 = jnp.float32
BF16 = jnp.bfloat16


def dot(a, b):
    return jnp.dot(a, b, preferred_element_type=F32)


def dot_nt(a, b):
    return lax.dot_general(a, b, (((1,), (1,)), ((), ())), preferred_element_type=F32)


def iota(shape, dim):
    return lax.broadcasted_iota(jnp.int32, shape, dim)


def deblur_kernel(
    devices_x, devices_y, planes, ext_x, views,
    est_ref, planes_ref, rows_ref, kidx_ref, psf_ref, out_ref,
    table, kz_small, kx_small, kz_wide, kx_wide, wy, kf, kt,
    cur, cbuf, zcat, blur, rim, rim_send, rim_recv, qext, q_send, q_recv, u, part, part_recv, meas, arrived,
    send_sem, recv_sem, plane_send_sem, plane_recv_sem,
):
    zx = planes * ext_x
    ny = est_ref.shape[1]
    taps = psf_ref.shape[1]
    rad = (taps - 1) // 2
    half = zx // 2
    gx = lax.axis_index("gx")
    gy = lax.axis_index("gy")
    has = {
        "left": gx > 0,
        "right": gx < devices_x - 1,
        "down": gy > 0,
        "up": gy < devices_y - 1,
    }
    to = {
        "left": (gx - 1, gy),
        "right": (gx + 1, gy),
        "down": (gx, gy - 1),
        "up": (gx, gy + 1),
    }
    slot_of = {"left": 0, "right": 1, "down": 0, "up": 1}
    back = {"left": "right", "right": "left", "down": "up", "up": "down"}

    devices = devices_x * devices_y
    me = gx * devices_y + gy

    def partner(k):
        other = lax.rem(me + k, devices)
        return other, (other // devices_y, lax.rem(other, devices_y))

    barrier = pltpu.get_barrier_semaphore()

    def greet(k, carry):
        pl.semaphore_signal(barrier, inc=1, device_id=partner(k)[1], device_id_type=MESH)
        return carry

    lax.fori_loop(1, devices, greet, 0)

    def send(side, kind, src, dst):
        num = kind * 2 + slot_of[side]

        @pl.when(has[side])
        def _():
            pltpu.make_async_remote_copy(
                src_ref=src, dst_ref=dst, send_sem=send_sem.at[num],
                recv_sem=recv_sem.at[kind * 2 + slot_of[side]],
                device_id=to[side], device_id_type=MESH,
            ).start()

    def wait_send(side, kind, src):
        num = kind * 2 + slot_of[side]

        @pl.when(has[side])
        def _():
            pltpu.make_async_remote_copy(
                src_ref=src, dst_ref=src, send_sem=send_sem.at[num], recv_sem=recv_sem.at[num],
                device_id=to[side], device_id_type=MESH,
            ).wait_send()

    def wait_recv(side, kind, dst):
        num = kind * 2 + slot_of[back[side]]

        @pl.when(has[side])
        def _():
            pltpu.make_async_remote_copy(
                src_ref=dst, dst_ref=dst, send_sem=send_sem.at[num], recv_sem=recv_sem.at[num],
                device_id=to[side], device_id_type=MESH,
            ).wait_recv()

    def clear_missing(side, dst):
        @pl.when(jnp.logical_not(has[side]))
        def _():
            dst[...] = jnp.zeros(dst.shape, dst.dtype)

    cur[...] = est_ref[...]
    cbuf[0, 1] = cur[...].astype(BF16)
    for it in range(ITERS):
        clear_missing("left", cbuf.at[it, 0])
        clear_missing("right", cbuf.at[it, 2])
        for kind_buf in (rim_recv, q_recv):
            clear_missing("down", kind_buf.at[it, 0])
            clear_missing("up", kind_buf.at[it, 1])
        clear_missing("left", part_recv.at[it, 0])
        clear_missing("right", part_recv.at[it, 1])

    def send_current(it):
        send("left", 4 * it, cbuf.at[it, 1], cbuf.at[it, 2])
        send("right", 4 * it, cbuf.at[it, 1], cbuf.at[it, 0])

    stride = next(s for s in (37, 41, 43, 47) if devices % s)
    share = -(-(devices - 1) // (6 * views))

    def send_planes(step):
        for j in range(share):
            turn = step * share + j + 1

            @pl.when(turn < devices)
            def _(turn=turn):
                k = lax.rem(turn * stride, devices)
                other, where = partner(k)
                pltpu.make_async_remote_copy(
                    src_ref=planes_ref.at[other], dst_ref=arrived.at[k],
                    send_sem=plane_send_sem, recv_sem=plane_recv_sem,
                    device_id=where, device_id_type=MESH,
                ).start()

    def all_planes():
        return pltpu.make_async_remote_copy(
            src_ref=arrived.at[pl.ds(1, devices - 1)], dst_ref=arrived.at[pl.ds(1, devices - 1)],
            send_sem=plane_send_sem, recv_sem=plane_recv_sem,
            device_id=partner(1)[1], device_id_type=MESH,
        )

    weights = psf_ref[...]
    weights = weights / jnp.sum(weights, axis=1, keepdims=True)
    tap = iota((taps, 128), 0)
    lane = iota((taps, 128), 1)

    def spread_taps(distance):
        select = (lane == jnp.where(distance < 0, distance + 128, distance)).astype(F32)
        return jnp.dot(weights, select, precision=lax.Precision.HIGHEST, preferred_element_type=F32)

    blocks = [tap - rad, rad - tap]
    blocks += [tap - rad - o for o in (-ext_x, 0, ext_x)]
    blocks += [rad + o - tap for o in (-ext_x, 0, ext_x)]
    for num, distance in enumerate(blocks):
        table[num] = spread_taps(distance)
    rounded = table[1].astype(BF16).astype(F32)
    scale = 1.0 / jnp.sum(rounded, axis=1, keepdims=True)
    table[8] = jnp.broadcast_to(scale, (scale.shape[0], 128))

    def toeplitz(base, count):
        return pltpu.roll(jnp.broadcast_to(base, (count, 128)), 0, 1, stride=1, stride_axis=0)

    def two_parts(matrix, width):
        where = iota(matrix.shape, 1)
        low = matrix - matrix.astype(BF16).astype(F32)
        return jnp.where(where < width, matrix, pltpu.roll(low, width, 1)).astype(BF16)

    for i in range(3):
        brick_x = jnp.clip(gx + (i - 1), 0, devices_x - 1)
        for v in range(views):
            n = i * views + v
            first = ((brick_x * devices_y + gy) * views + v) * 3
            id_x, id_y, id_z = (kidx_ref[first + e] for e in range(3))
            factor = table[8, pl.ds(id_y, 1), :]
            for way in range(2):
                base = table[way, pl.ds(id_z, 1), :] * factor
                at = (way * 3 * views + n) * planes
                kz_small[at:at + planes, :] = two_parts(toeplitz(base, planes), planes)
                block = 2 + 3 * way + i
                base = table[block, pl.ds(id_x, 1), :]
                at = (way * 3 * views + n) * ext_x
                kx_small[at:at + ext_x, :] = two_parts(toeplitz(base, ext_x), ext_x)
            ring = toeplitz(table[1, pl.ds(id_y, 1), :], ny)
            apart = iota((ny, 128), 1) - iota((ny, 128), 0)
            near = (apart >= -rad) & (apart <= rad)
            wy[v, i * ny:(i + 1) * ny, 0:128] = jnp.where(near, ring, 0.0).astype(BF16)
            edge = jnp.where(near, 0.0, ring)
            if v:
                edge = pltpu.roll(edge, 32 * v, 1)
            wy[v, i * ny:(i + 1) * ny, 128:256] = edge.astype(BF16)

    pl.semaphore_wait(barrier, devices - 1)
    send_current(0)
    arrived[0] = planes_ref[me]

    wide = (128, zx)
    row = iota(wide, 0)
    col = iota(wide, 1)
    col_z = col // ext_x
    col_x = lax.rem(col, ext_x)
    pick_z = ((row == col_z) | (row == col_z + planes)).astype(F32).astype(BF16)
    pick_x = ((row == col_x) | (row == col_x + ext_x)).astype(F32).astype(BF16)

    def expand(n, carry):
        at = pl.multiple_of(n * 96, 32)
        res = dot(kz_small[pl.ds(at, 96), :], pick_z)
        for part_num in range(zx // 128):
            kz_wide[part_num, pl.ds(at, 96), :] = res[:, part_num * 128:(part_num + 1) * 128]
        return carry

    lax.fori_loop(0, kz_small.shape[0] // 96, expand, 0)
    kx_wide[...] = dot(kx_small[...], pick_x[:, 0:128])

    def build(way):
        def one(n, carry):
            if way == 0:
                send_planes(n)
            i = n // views
            v = lax.rem(n, views)
            num = way * 3 * views + n
            tile = kx_wide[pl.ds(pl.multiple_of(num * ext_x, 16), ext_x), :]
            for z in range(planes):
                for b in range(zx // 128):
                    line = kz_wide[b, pl.ds(num * planes + z, 1), :]
                    value = (jnp.broadcast_to(line, (ext_x, 128)) * tile).astype(BF16)
                    if way == 0:
                        at = pl.multiple_of(v * zx + z * ext_x, 16)
                        kf[i, pl.ds(at, ext_x), b * 128:(b + 1) * 128] = value
                    else:
                        at = pl.multiple_of(v * zx + b * 128, 128)
                        kt[i, z * ext_x:(z + 1) * ext_x, pl.ds(at, 128)] = value
            return carry

        lax.fori_loop(0, 3 * views, one, 0)

    build(0)

    lane_half = iota((half, 128), 1)
    low_half = lax.rem(lane_half, 32) < 16

    def fold(value, first):
        top, bottom = value[0:half], value[half:zx]
        if first:
            return jnp.where(low_half, top, pltpu.roll(bottom, 16, 1)).astype(BF16)
        return jnp.where(low_half, pltpu.roll(bottom, 112, 1), top).astype(BF16)

    def unfold(from_first, from_second):
        a, b = from_first.astype(F32), from_second.astype(F32)
        top = jnp.where(low_half, a, b)
        bottom = jnp.where(low_half, pltpu.roll(a, 112, 1), pltpu.roll(b, 16, 1))
        return top, bottom

    def forward_zx(it, i):
        def one(v, carry):
            if it == 0:
                send_planes((3 + (1, 0, 2)[i]) * views + v)
            at = pl.multiple_of(v * zx, zx)
            zcat[pl.ds(at, zx), i * ny:(i + 1) * ny] = dot(
                kf[i, pl.ds(at, zx), :], cbuf[it, i]
            ).astype(BF16)
            return carry

        lax.fori_loop(0, views, one, 0)

    def forward_y():
        rim[...] = jnp.zeros(rim.shape, F32)

        def one(v, carry):
            at = pl.multiple_of(v * zx, zx)
            res = dot(zcat[pl.ds(at, zx), :], wy[v])
            blur[pl.ds(at, zx), :] = res[:, 0:128]
            rim[...] += res[:, 128:256]
            return carry

        lax.fori_loop(0, views, one, 0)

    def adjoint_y():
        def one(v, carry):
            at = pl.multiple_of(v * zx, zx)
            res = dot_nt(qext[pl.ds(at, zx), :], wy[v]).astype(BF16)
            for i in range(3):
                u[i, pl.ds(at, zx), :] = res[:, i * ny:(i + 1) * ny]
            return carry

        lax.fori_loop(0, views, one, 0)

    lane_q = iota((zx, 128), 1)
    low_q = lax.rem(lane_q, 32) < 16

    for it in range(ITERS):
        kind_c, kind_rim, kind_q, kind_p = (4 * it + k for k in range(4))
        forward_zx(it, 1)
        wait_recv("left", kind_c, cbuf.at[it, 0])
        wait_recv("right", kind_c, cbuf.at[it, 2])
        forward_zx(it, 0)
        forward_zx(it, 2)
        forward_y()
        rim_send[it, 1] = fold(rim[...], True)
        rim_send[it, 0] = fold(rim[...], False)
        send("up", kind_rim, rim_send.at[it, 1], rim_recv.at[it, 0])
        send("down", kind_rim, rim_send.at[it, 0], rim_recv.at[it, 1])
        if it == 0:
            build(1)

            all_planes().wait_recv()

            def take(p, carry):
                place = rows_ref[p]
                at = pl.ds(pl.multiple_of(p * ext_x, ext_x), ext_x)
                meas[at, :] = arrived[place // 2, lax.rem(place, 2)]
                return carry

            lax.fori_loop(0, views * planes, take, 0)
        wait_recv("down", kind_rim, rim_recv.at[it, 0])
        wait_recv("up", kind_rim, rim_recv.at[it, 1])
        tops = unfold(rim_recv[it, 0], rim_recv[it, 1])
        rim[0:half] = tops[0]
        rim[half:zx] = tops[1]
        packed = jnp.zeros((zx, 128), F32)
        for v in range(views):
            add = rim[...]
            if v:
                add = pltpu.roll(add, 128 - 32 * v, 1)
            edge = (lane_q < rad) | (lane_q >= 128 - rad)
            total = blur[v * zx:(v + 1) * zx, :] + jnp.where(edge, add, 0.0)
            q = meas[v * zx:(v + 1) * zx, :].astype(F32) / total
            qext[v * zx:(v + 1) * zx, 0:128] = q.astype(BF16)
            moved = pltpu.roll(q, 32 * v, 1) if v else q
            place = lax.rem(lane_q - 32 * v + 128 + rad, 128)
            packed = jnp.where(place < 2 * rad, moved, packed)
        q_send[it, 0] = fold(packed, True)
        q_send[it, 1] = fold(packed, False)
        send("down", kind_q, q_send.at[it, 0], q_recv.at[it, 1])
        send("up", kind_q, q_send.at[it, 1], q_recv.at[it, 0])
        wait_recv("down", kind_q, q_recv.at[it, 0])
        wait_recv("up", kind_q, q_recv.at[it, 1])
        tops = unfold(q_recv[it, 1], q_recv[it, 0])
        for v in range(views):
            qext[v * zx:v * zx + half, 128:256] = tops[0].astype(BF16)
            qext[v * zx + half:(v + 1) * zx, 128:256] = tops[1].astype(BF16)
        adjoint_y()
        part[it, 0] = dot(kt[0], u[0])
        send("left", kind_p, part.at[it, 0], part_recv.at[it, 1])
        part[it, 1] = dot(kt[2], u[2])
        send("right", kind_p, part.at[it, 1], part_recv.at[it, 0])
        own = dot(kt[1], u[1])
        wait_recv("left", kind_p, part_recv.at[it, 0])
        wait_recv("right", kind_p, part_recv.at[it, 1])
        correction = (own + part_recv[it, 0] + part_recv[it, 1]) * (1.0 / views)
        updated = cur[...] * correction
        if it < ITERS - 1:
            cur[...] = updated
            cbuf[it + 1, 1] = updated.astype(BF16)
            send_current(it + 1)
        else:
            out_ref[...] = updated

    all_planes().wait_send()
    for it in range(ITERS):
        kind_c, kind_rim, kind_q, kind_p = (4 * it + k for k in range(4))
        for side in ("left", "right"):
            wait_send(side, kind_c, cbuf.at[it, 1])
            wait_send(side, kind_p, part.at[it, 0])
        for side in ("down", "up"):
            wait_send(side, kind_rim, rim_send.at[it, 0])
            wait_send(side, kind_q, q_send.at[it, 0])


def exchange(stored, placement, devices):
    slots = stored.shape[0]
    me = lax.axis_index("gx") * lax.axis_size("gy") + lax.axis_index("gy")
    slot = jnp.arange(slots, dtype=jnp.int32)[None, :]
    own = lax.dynamic_slice_in_dim(placement, me * slots, slots) // slots
    match = own[None, :] == jnp.arange(devices, dtype=jnp.int32)[:, None]
    first = jnp.min(jnp.where(match, slot, slots - 1), axis=1)
    last = jnp.max(jnp.where(match, slot, 0), axis=1)
    source = jnp.stack([first, last], axis=1).reshape(-1)
    outgoing = jnp.take(stored, source, axis=0, mode="clip")
    outgoing = outgoing.reshape((devices, 2) + stored.shape[1:])
    everything = placement.reshape(devices, slots)
    wanted = everything // slots == me
    item = everything % slots
    first = jnp.min(jnp.where(wanted, slot, slots), axis=1, keepdims=True)
    last = jnp.max(jnp.where(wanted, slot, -1), axis=1, keepdims=True)
    item_first = jnp.max(jnp.where(slot == first, item, -1), axis=1)
    item_last = jnp.max(jnp.where((slot == last) & (last > first), item, -1), axis=1)
    items = jnp.arange(slots, dtype=jnp.int32)[:, None]
    origin = (me - jnp.arange(devices, dtype=jnp.int32)[None, :]) % devices
    row = jnp.max(
        jnp.where(item_first[None, :] == items, 2 * origin, 0)
        + jnp.where(item_last[None, :] == items, 2 * origin + 1, 0),
        axis=1,
    )
    return outgoing, row


def solution(mesh):
    devices_x, devices_y = mesh.shape["gx"], mesh.shape["gy"]

    def shards(estimate, stored, placement, psf_taps, kernel_index):
        planes, ext_x, ny = estimate.shape
        zx = planes * ext_x
        views = kernel_index.shape[2]
        outgoing, row = exchange(stored, placement, devices_x * devices_y)
        vmem = pl.BlockSpec(memory_space=pltpu.VMEM)
        smem = pl.BlockSpec(memory_space=pltpu.SMEM)
        n = 3 * views
        half = zx // 2
        refined = pl.pallas_call(
            functools.partial(deblur_kernel, devices_x, devices_y, planes, ext_x, views),
            out_shape=jax.ShapeDtypeStruct((zx, ny), F32),
            in_specs=[vmem, vmem, smem, smem, vmem],
            out_specs=vmem,
            scratch_shapes=[
                pltpu.VMEM((9, psf_taps.shape[0], 128), F32),
                pltpu.VMEM((2 * n * planes, 128), BF16),
                pltpu.VMEM((2 * n * ext_x, 128), BF16),
                pltpu.VMEM((zx // 128, 2 * n * planes, 128), F32),
                pltpu.VMEM((2 * n * ext_x, 128), F32),
                pltpu.VMEM((views, 3 * ny, 256), BF16),
                pltpu.VMEM((3, views * zx, zx), BF16),
                pltpu.VMEM((3, zx, views * zx), BF16),
                pltpu.VMEM((zx, ny), F32),
                pltpu.VMEM((ITERS, 3, zx, ny), BF16),
                pltpu.VMEM((views * zx, 3 * ny), BF16),
                pltpu.VMEM((views * zx, ny), F32),
                pltpu.VMEM((zx, 128), F32),
                pltpu.VMEM((ITERS, 2, half, 128), BF16),
                pltpu.VMEM((ITERS, 2, half, 128), BF16),
                pltpu.VMEM((views * zx, 256), BF16),
                pltpu.VMEM((ITERS, 2, half, 128), BF16),
                pltpu.VMEM((ITERS, 2, half, 128), BF16),
                pltpu.VMEM((3, views * zx, ny), BF16),
                pltpu.VMEM((ITERS, 2, zx, ny), F32),
                pltpu.VMEM((ITERS, 2, zx, ny), F32),
                pltpu.VMEM((views * zx, ny), BF16),
                pltpu.VMEM(outgoing.shape, BF16),
                pltpu.SemaphoreType.DMA((8 * ITERS,)),
                pltpu.SemaphoreType.DMA((8 * ITERS,)),
                pltpu.SemaphoreType.DMA,
                pltpu.SemaphoreType.DMA,
            ],
            compiler_params=pltpu.CompilerParams(
                collective_id=0, has_side_effects=True, vmem_limit_bytes=60 * 1024 * 1024
            ),
        )(
            estimate.reshape(zx, ny),
            outgoing,
            row,
            kernel_index.reshape(-1),
            psf_taps,
        )
        return refined.reshape(planes, ext_x, ny)

    return jax.shard_map(
        shards,
        mesh=mesh,
        in_specs=(P(None, "gx", "gy"), P(("gx", "gy"), None, None), P(), P(), P()),
        out_specs=P(None, "gx", "gy"),
        check_vma=False,
    )
```
